256 devices in a mesh: ctx: 64 (over z, y, x_lo), head: 4 (over x_hi, core).
Axes of the slice: x: 4 (x_hi: 2, x_lo: 2; x = x_hi * 2 + x_lo), y: 4, z: 8, core: 2. Of those that a mesh axis runs over, the one named last changes fastest.
Arguments:
- q_nope: bfloat16 [8192, 64, 128], P('ctx', 'head'), may hold values from -6 to 6
- q_rope: bfloat16 [8192, 4096], P('ctx', 'head'), may hold values from -80 to 80
- latent: bfloat16 [8192, 576], P('ctx'), may hold values from -4 to 4
- positions: int32 [8192], P('ctx'), may hold values from 0 to 8191, each once
- w_uk: bfloat16 [64, 128, 512], P('head'), may hold values from -0.5 to 0.5
- w_uv: bfloat16 [64, 512, 128], P('head'), may hold values from -0.25 to 0.25
- w_o: bfloat16 [8192, 3584], P('head', 'ctx'), may hold values from -0.5 to 0.5
Outputs:
- projected: bfloat16 [8192, 3584], P(('ctx', 'head'))
The draws below stay inside these ranges and needn't reach their ends.
Inputs may be any that keep to these rules, and one draw needn't show every extreme that they name: positions holds each of 0 to 8191 once.
All inputs are finite; a program needn't handle non-finite values.
Results may differ from the reference program's by a relative error of at most 0.015.
Values may be sent and summed in bfloat16 or wider, within the bound.
No kernel may reach another device: no remote copies, remote signals or barrier semaphores. Data moves between devices by JAX's collectives and lax.ppermute only.
A program may use at most 128 MiB of HBM per device.

```python
import jax
import jax.numpy as jnp
from jax import lax

D = 3584
LAT = 512
ROPE = 64
NOPE = 128
VH = 128
HEADS = 64
T_DEV = 128
STEPS = 16
HEADS_DEV = 16
SEQ = 8192
N_HEAD = 4


def shared_latent(key):
    base = jax.random.fold_in(key, 7)
    values = jnp.clip(jax.random.normal(base, (SEQ, LAT + ROPE), jnp.float32), -4.0, 4.0)
    return values


def draw_latent(key, part):
    return shared_latent(key).astype(jnp.bfloat16)


def draw_q_rope(key, part):
    base = jax.random.fold_in(key, 13)
    values = jnp.clip(jax.random.normal(base, (SEQ, HEADS, ROPE), jnp.float32), -4.0, 4.0)
    return values.reshape(SEQ, HEADS * ROPE).astype(jnp.bfloat16)


def steps_of(own_key, extent, shards, low, high):
    factor_of = 1.0
    for axis_at, blocks in shards:
        heights = jax.random.uniform(jax.random.fold_in(jax.random.fold_in(own_key, 6), axis_at), (blocks,), jnp.float32, low / len(shards), high / len(shards))
        factor_of = factor_of * jnp.repeat(jnp.exp(heights), extent[axis_at] // blocks).reshape((-1,) + (1,) * (len(extent) - 1 - axis_at))
    return factor_of


def scatter_about(rng, dims, spread, most, split=(), kind=jnp.bfloat16):
    values = jax.random.normal(rng, dims, jnp.float32) * spread
    if len(split) > 0:
        values = steps_of(rng, dims, split, -0.22, 0.18) * values
    return jnp.clip(values, min=-most, max=most).astype(kind)


def setup_inputs(seed: int = 0) -> dict:
    arg_keys = jax.random.split(jax.random.key(seed), 8)
    q_nope = scatter_about(arg_keys[0], (SEQ, HEADS, NOPE), 1.0, 6.0, ((0, 64), (1, 4)))
    q_rope = draw_q_rope(jax.random.fold_in(arg_keys[7], 71), 0)
    latent = draw_latent(jax.random.fold_in(arg_keys[7], 71), 0)
    positions = jax.random.permutation(arg_keys[3], SEQ).astype(jnp.int32)
    w_uk = scatter_about(arg_keys[4], (HEADS, NOPE, LAT), NOPE ** -0.5, 0.5, ((0, 4),))
    w_uv = scatter_about(arg_keys[5], (HEADS, LAT, VH), LAT ** -0.5, 0.25, ((0, 4),))
    w_o = scatter_about(arg_keys[6], (HEADS * VH, D), (HEADS * VH // 64) ** -0.5, 0.5, ((0, 4), (1, 64)))
    return dict(q_nope=q_nope, q_rope=q_rope, latent=latent, positions=positions, w_uk=w_uk, w_uv=w_uv, w_o=w_o)


def reference(q_nope, q_rope, latent, positions, w_uk, w_uv, w_o):
    blocks = SEQ // T_DEV
    scale = (NOPE + ROPE) ** -0.5
    q_latent = jnp.einsum('thn,hnl->thl', q_nope.astype(jnp.float32), w_uk.astype(jnp.float32)).astype(jnp.bfloat16)
    q_rot = q_rope.reshape(SEQ, HEADS, ROPE)
    lat_blocks = latent.reshape(blocks, T_DEV, LAT + ROPE)
    pos_blocks = positions.reshape(blocks, T_DEV)

    def one_block(index):
        start = (index * T_DEV).astype(jnp.int32)
        q_lat = lax.dynamic_slice_in_dim(q_latent, start, T_DEV, 0).astype(jnp.float32)
        q_rp = lax.dynamic_slice_in_dim(q_rot, start, T_DEV, 0).astype(jnp.float32)
        q_pos = lax.dynamic_slice_in_dim(positions, start, T_DEV, 0)
        chosen = ((index - jnp.arange(STEPS, dtype=jnp.int32)) % blocks).astype(jnp.int32)
        keys = lat_blocks[chosen].reshape(STEPS * T_DEV, LAT + ROPE).astype(jnp.float32)
        key_pos = pos_blocks[chosen].reshape(STEPS * T_DEV)
        scores = jnp.einsum('thl,kl->thk', q_lat, keys[:, :LAT]) + jnp.einsum('thr,kr->thk', q_rp, keys[:, LAT:])
        scores = scores * scale
        visible = key_pos[None, None, :] <= q_pos[:, None, None]
        scores = jnp.where(visible, scores, -jnp.inf)
        top = jnp.max(scores, axis=-1, keepdims=True)
        weights = jnp.exp(scores - top)
        total = jnp.sum(weights, axis=-1)
        weights_b = weights.astype(jnp.bfloat16).astype(jnp.float32)
        summed = jnp.einsum('thk,kl->thl', weights_b, keys[:, :LAT])
        return (summed / total[:, :, None]).astype(jnp.bfloat16)

    o_latent = lax.map(one_block, jnp.arange(blocks, dtype=jnp.int32)).reshape(SEQ, HEADS, LAT)
    head_out = jnp.einsum('thl,hlv->thv', o_latent.astype(jnp.float32), w_uv.astype(jnp.float32)).astype(jnp.bfloat16)
    head_out = head_out.reshape(SEQ, HEADS * VH)
    width = HEADS_DEV * VH
    result = jnp.zeros((SEQ, D), jnp.float32)
    for group in range(N_HEAD):
        part = jnp.dot(head_out[:, group * width:(group + 1) * width], w_o[group * width:(group + 1) * width], preferred_element_type=jnp.float32)
        result = result + lax.optimization_barrier(part.astype(jnp.bfloat16)).astype(jnp.float32)
    return result.astype(jnp.bfloat16)
```

```python
import functools
import math

import jax
import jax.numpy as jnp
from jax import lax
from jax.experimental import pallas as pl
from jax.experimental.pallas import tpu as pltpu
from jax.sharding import Mesh, PartitionSpec as P


CTX = ("z", "y", "xl")
HEAD = ("xh", "core")
LANES = 640
NT = (((1,), (1,)), ((), ()))
BF16, F32 = jnp.bfloat16, jnp.float32


def shift(x, axis, by):
    n = lax.axis_size(axis)
    return lax.ppermute(x, axis, [(i, (i + by) % n) for i in range(n)])


def attend(first, last, scale, nkv, *refs):
    q_ref, qpos_ref, sel_ref = refs[:3]
    kv_refs = refs[3 : 3 + nkv]
    at = 3 + nkv
    if not first:
        ml_ref, acc_ref = refs[at : at + 2]
        at += 2
    if last:
        uv_ref = refs[at]
        at += 1
    outs = refs[at:]
    kv = kv_refs[0][...] if nkv == 1 else jnp.concatenate([r[...] for r in kv_refs], axis=0)
    rows = q_ref.shape[0]
    lat = acc_ref.shape[1] if not first else outs[1].shape[1]
    c = scale * math.log2(math.e)
    key_pos = lax.dot_general(sel_ref[...], kv, NT, preferred_element_type=F32)[0:1, :]
    toks = qpos_ref.shape[0]
    bias = jnp.where(key_pos <= qpos_ref[...], 0.0, -jnp.inf)
    n = kv.shape[0]
    s = lax.dot_general(q_ref[...], kv, NT, preferred_element_type=F32)
    s = (s.reshape(rows // toks, toks, n) + bias[None]).reshape(rows, n)
    top = jnp.max(s, axis=1, keepdims=True)
    if not first:
        m_old = ml_ref[:, 0:1]
        l_old = ml_ref[:, 64:65]
        top = jnp.maximum(top, m_old)
    p = jnp.exp2(s * c - top * c)
    total = jnp.sum(p, axis=1, keepdims=True)
    o = jnp.dot(p.astype(BF16), kv[:, :lat], preferred_element_type=F32)
    if not first:
        alpha = jnp.exp2(m_old * c - top * c)
        total = total + l_old * alpha
        o = o + acc_ref[...] * alpha
    if not last:
        half = lax.broadcasted_iota(jnp.int32, (rows, 128), 1) < 64
        outs[0][...] = jnp.where(half, top, total)
        outs[1][...] = o
    else:
        o = (o / total).astype(BF16)
        for h in range(rows // toks):
            v = jnp.dot(
                o[h * toks : (h + 1) * toks], uv_ref[h], preferred_element_type=F32
            )
            outs[0][:, h * v.shape[1] : (h + 1) * v.shape[1]] = v.astype(BF16)


def attention(q, qpos, sel, kvs, state, w_uv, scale, lat, base, tiles, rt, name):
    first, last = state is None, w_uv is not None
    toks = qpos.shape[0]
    whole = lambda a: pl.BlockSpec(a.shape, lambda i: (0,) * a.ndim)
    row = lambda w: pl.BlockSpec((rt, w), lambda i: (i + base, 0))
    args = [q, qpos, sel, *kvs]
    specs = [row(q.shape[1]), whole(qpos), whole(sel), *[whole(k) for k in kvs]]
    if not first:
        args += list(state)
        specs += [row(128), row(lat)]
    if last:
        hp = rt // toks
        vh = w_uv.shape[2]
        args.append(w_uv)
        specs.append(pl.BlockSpec((hp, lat, vh), lambda i: (i + base, 0, 0)))
        out_shape = (jax.ShapeDtypeStruct((toks, tiles * hp * vh), BF16),)
        out_specs = (pl.BlockSpec((toks, hp * vh), lambda i: (0, i)),)
    else:
        out_shape = (
            jax.ShapeDtypeStruct((q.shape[0], 128), F32),
            jax.ShapeDtypeStruct((q.shape[0], lat), F32),
        )
        out_specs = (row(128), row(lat))
    n = sum(k.shape[0] for k in kvs)
    r = tiles * rt
    return pl.pallas_call(
        functools.partial(attend, first, last, scale, len(kvs)),
        out_shape=out_shape,
        grid=(tiles,),
        in_specs=specs,
        out_specs=out_specs,
        cost_estimate=pl.CostEstimate(
            flops=2 * r * n * (LANES + lat), bytes_accessed=r * 6 * lat, transcendentals=r * n
        ),
        name=name,
    )(*args)


def local(q_nope, q_rope, latent, positions, w_uk, w_uv, w_o):
    toks, heads, nope = q_nope.shape
    lat = w_uk.shape[2]
    rope = q_rope.shape[1] // heads
    scale = (nope + rope) ** (-0.5)
    core, xh, y, z = (lax.axis_index(a) for a in ("core", "xh", "y", "z"))
    nz, ny, nxl = lax.axis_size("z"), lax.axis_size("y"), lax.axis_size("xl")
    half = toks // 2

    block = jnp.concatenate(
        [
            latent,
            (positions // 64).astype(BF16)[:, None],
            (positions % 64).astype(BF16)[:, None],
            jnp.zeros((toks, LANES - lat - rope - 2), BF16),
        ],
        axis=1,
    )
    mine = lax.dynamic_slice_in_dim(block, core * half, half, 0)
    have = mine
    groups = []
    for by in (1, 2, 4, 8):
        got = shift(have, CTX, by)
        other = shift(got, "core", 1)
        groups.append((got, other))
        have = jnp.concatenate([have, got], axis=0)

    wt = w_o.T
    cols = wt.shape[0]
    xl = lax.axis_index("xl")
    w_other = shift(wt, "xl", 1)
    pair = jnp.where(xl == 0, jnp.stack([wt, w_other]), jnp.stack([w_other, wt]))
    pair = pair.reshape(1, nxl * cols, wt.shape[1])
    w_all = jnp.zeros((nz, nxl * cols, wt.shape[1]), BF16)
    put = lambda acc, piece, at: lax.dynamic_update_slice(acc, piece, (at % nz, 0, 0))
    w_all = put(w_all, pair, z)
    up = down = pair
    for s in range(1, nz // 2 + 1):
        down = shift(down, "z", -1)
        w_all = put(w_all, down, z + s)
        if s < nz // 2:
            up = shift(up, "z", 1)
            w_all = put(w_all, up, z - s + nz)

    q_lat = jnp.einsum("thn,hnl->htl", q_nope, w_uk, preferred_element_type=F32).astype(BF16)
    q_rot = q_rope.reshape(toks, heads, rope).transpose(1, 0, 2)
    q = jnp.concatenate(
        [q_lat, q_rot, jnp.zeros((heads, toks, LANES - lat - rope), BF16)], axis=2
    ).reshape(heads * toks, LANES)
    qpos = positions.astype(F32)[:, None]
    lane = lax.broadcasted_iota(jnp.int32, (16, LANES), 1)
    sel = jnp.where(lane == lat + rope, 64.0, jnp.where(lane == lat + rope + 1, 1.0, 0.0)).astype(BF16)

    rt = 4 * toks
    tiles = heads * toks // rt
    call = functools.partial(attention, q, qpos, sel, scale=scale, lat=lat, rt=rt)
    state = call([block, *groups[0]], None, None, base=0, tiles=tiles, name="attend_a")
    state = call(list(groups[1]), state, None, base=0, tiles=tiles, name="attend_b")
    state = call(list(groups[2]), state, None, base=0, tiles=tiles, name="attend_c")
    halves = []
    for part in range(2):
        (h,) = call(
            list(groups[3]), state, w_uv, base=part * tiles // 2, tiles=tiles // 2, name=f"attend_d{part}"
        )
        halves.append(jnp.stack([h] + [shift(h, "y", r) for r in range(1, ny)]))

    hv = jnp.concatenate(halves, axis=2).reshape(ny * toks, -1)
    wf = w_all.reshape(nz * nxl * cols, -1)
    part = lax.dot_general(hv, wf, NT, preferred_element_type=F32)
    rows = toks // 4
    part = part.reshape(ny, 2, 2, rows, -1)
    pick = lambda a, i, ax: lax.dynamic_index_in_dim(a, i, ax, keepdims=False)
    keep, give = pick(part, core, 2), pick(part, 1 - core, 2).astype(BF16)
    both = keep + shift(give, "core", 1).astype(F32)
    keep, give = pick(both, xh, 1), pick(both, 1 - xh, 1).astype(BF16)
    done = (keep + shift(give, "xh", 1).astype(F32)).astype(BF16)
    pieces = jnp.stack([done[0]] + [shift(done[r], "y", -r) for r in range(1, ny)])
    pieces = jnp.concatenate([pieces, pieces], axis=0)
    pieces = lax.dynamic_slice_in_dim(pieces, (ny - y) % ny, ny, 0)
    out = pieces.reshape(ny, rows, nz, nxl * cols).transpose(1, 2, 0, 3)
    return out.reshape(rows, nz * ny * nxl * cols)


def solution(mesh):
    fine = Mesh(mesh.devices.reshape(8, 4, 2, 2, 2), (*CTX, *HEAD))
    placed = (
        P(CTX, HEAD, None),
        P(CTX, HEAD),
        P(CTX, None),
        P(CTX),
        P(HEAD, None, None),
        P(HEAD, None, None),
        P(HEAD, CTX),
    )
    return jax.shard_map(
        local, mesh=fine, in_specs=placed, out_specs=P((*CTX, *HEAD), None), check_vma=False
    )
```

```python
import functools
import math

import jax
import jax.numpy as jnp
from jax import lax
from jax.experimental import pallas as pl
from jax.experimental.pallas import tpu as pltpu
from jax.sharding import Mesh, PartitionSpec as P


CTX = ("z", "y", "xl")
HEAD = ("xh", "core")
LANES = 640
TILE = 512
NT = (((1,), (1,)), ((), ()))
TN = (((0,), (0,)), ((), ()))
BF16, F32 = jnp.bfloat16, jnp.float32
VMEM = pl.BlockSpec(memory_space=pltpu.VMEM)
SMEM = pl.BlockSpec(memory_space=pltpu.SMEM)


def shift(x, axis, by):
    n = lax.axis_size(axis)
    return lax.ppermute(x, axis, [(i, (i + by) % n) for i in range(n)])


def params(mib=24):
    return pltpu.CompilerParams(vmem_limit_bytes=mib << 20)


def attend(first, last, scale, nkv, *refs):
    q_ref, qpos_ref = refs[:2]
    kv_refs = refs[2 : 2 + nkv]
    at = 2 + nkv
    if not first:
        ml_in, acc_in = refs[at : at + 2]
        at += 2
    if last:
        uv_ref, h_ref, k_ref, kt_ref, sa_ref, sb_ref = refs[at:]
    else:
        ml_out, acc_out, k_ref, kt_ref, sa_ref, sb_ref = refs[at:]
    lat = kt_ref.shape[0]
    toks = qpos_ref.shape[1]
    c = scale * math.log2(math.e)
    at = 0
    for r in kv_refs:
        n = r.shape[0]
        k_ref[at : at + n, :] = r[...]
        at += n
    n = at
    kt_ref[...] = k_ref[:, :lat].T
    tag = k_ref[:, LANES - 128 :].astype(F32)
    key_pos = tag[:, 64:65] * 64.0 + tag[:, 65:66]
    bias = jnp.where(key_pos <= qpos_ref[...], 0.0, -jnp.inf)
    bias = jnp.concatenate([bias] * (TILE // toks), axis=1)
    tiles = q_ref.shape[1] // TILE

    def at_tile(i):
        return pl.ds(pl.multiple_of(i * TILE, TILE), TILE)

    def score(i, s_ref):
        s_ref[...] = jnp.dot(k_ref[...], q_ref[:, at_tile(i)], preferred_element_type=F32) + bias

    def absorb(i, s_ref):
        cols = at_tile(i)
        s = s_ref[...]
        top = jnp.max(s, axis=0, keepdims=True)
        if not first:
            m_old = ml_in[0:1, cols]
            top = jnp.maximum(top, m_old)
        p = jnp.exp2(s * c - top * c)
        total = jnp.sum(p, axis=0, keepdims=True)
        o = jnp.dot(kt_ref[...], p.astype(BF16), preferred_element_type=F32)
        if not first:
            alpha = jnp.exp2(m_old * c - top * c)
            total = total + ml_in[1:2, cols] * alpha
            o = o + acc_in[:, cols] * alpha
        if not last:
            ml_out[0:1, cols] = top
            ml_out[1:2, cols] = total
            acc_out[:, cols] = o
        else:
            o = (o / total).astype(BF16)
            hp = TILE // toks
            vh = uv_ref.shape[2]
            for h in range(hp):
                v = lax.dot_general(
                    o[:, h * toks : (h + 1) * toks], uv_ref[i * hp + h], TN, preferred_element_type=F32
                )
                h_ref[:, pl.ds(pl.multiple_of((i * hp + h) * vh, vh), vh)] = v.astype(BF16)

    score(0, sa_ref)

    @pl.loop(0, tiles // 2)
    def _(j):
        score(2 * j + 1, sb_ref)
        absorb(2 * j, sa_ref)
        score(jnp.minimum(2 * j + 2, tiles - 2), sa_ref)
        absorb(2 * j + 1, sb_ref)


def attention(q, qpos, kvs, state, uvt, scale, lat, name):
    first, last = state is None, uvt is not None
    toks, rows = qpos.shape[1], q.shape[1]
    n = sum(k.shape[0] for k in kvs)
    args = [q, qpos, *kvs]
    alias = {}
    if not first:
        if not last:
            alias = {len(args): 0, len(args) + 1: 1}
        args += list(state)
    if last:
        args.append(uvt)
        out_shape = (jax.ShapeDtypeStruct((toks, uvt.shape[0] * uvt.shape[2]), BF16),)
    else:
        out_shape = (
            jax.ShapeDtypeStruct((8, rows), F32),
            jax.ShapeDtypeStruct((lat, rows), F32),
        )
    return pl.pallas_call(
        functools.partial(attend, first, last, scale, len(kvs)),
        out_shape=out_shape,
        in_specs=[VMEM] * len(args),
        out_specs=(VMEM,) * len(out_shape),
        scratch_shapes=[pltpu.VMEM((n, LANES), BF16), pltpu.VMEM((lat, n), BF16)]
        + [pltpu.VMEM((n, TILE), F32)] * 2,
        input_output_aliases=alias,
        compiler_params=params(),
        cost_estimate=pl.CostEstimate(
            flops=2 * rows * n * (LANES + lat), bytes_accessed=rows * lat, transcendentals=rows * n
        ),
        name=name,
    )(*args)


def gather_w(nz, *refs):
    at_ref, out_ref = refs[0], refs[-1]
    for j, r in enumerate(refs[1:-1]):
        n = r.shape[0]
        out_ref[pl.ds(pl.multiple_of(lax.rem(at_ref[3] + j, nz) * n, n), n), :] = r[...]


def project(k, *refs):
    at_ref = refs[0]
    h_refs = refs[1 : 1 + k]
    w_ref, keep_ref, give_ref, sums = refs[1 + k :]
    h = h_refs[0][...] if k == 1 else jnp.concatenate([r[...] for r in h_refs], axis=0)
    sums[...] = lax.dot_general(h, w_ref[...], NT, preferred_element_type=F32)
    core = at_ref[0]
    n = keep_ref.shape[2]
    for r in range(k):
        for x in range(2):
            base = (r * 4 + x * 2) * n
            keep_ref[r, x] = sums[pl.ds(pl.multiple_of(base + core * n, n), n), :]
            give_ref[r, x] = sums[pl.ds(pl.multiple_of(base + (1 - core) * n, n), n), :].astype(BF16)


def fold(at_ref, keep_ref, got_ref, keep2_ref, give_ref):
    xh = at_ref[1]
    for r in range(keep_ref.shape[0]):
        keep2_ref[r] = keep_ref[r, xh] + got_ref[r, xh].astype(F32)
        give_ref[r] = (keep_ref[r, 1 - xh] + got_ref[r, 1 - xh].astype(F32)).astype(BF16)


def finish(nz, ny, *refs):
    at_ref, out_ref, rows = refs[0], refs[-2], refs[-1]
    for r, p in enumerate(refs[1:-2]):
        rows[lax.rem(at_ref[2] + r, ny)] = p[...].astype(F32)
    w = rows.shape[2] // nz
    out_ref[...] = jnp.concatenate(
        [rows[y, :, z * w : (z + 1) * w] for z in range(nz) for y in range(ny)], axis=1
    ).astype(BF16)


def call(kern, args, outs, name, scratch=(), mib=24):
    outs = [jax.ShapeDtypeStruct(*o) for o in outs]
    return pl.pallas_call(
        kern,
        out_shape=outs,
        in_specs=[SMEM] + [VMEM] * (len(args) - 1),
        out_specs=[VMEM] * len(outs),
        scratch_shapes=list(scratch),
        compiler_params=params(mib),
        name=name,
    )(*args)


def local(q_nope, q_rope, latent, positions, w_uk, w_uv, w_o):
    toks, heads, nope = q_nope.shape
    lat = w_uk.shape[2]
    rope = q_rope.shape[1] // heads
    scale = (nope + rope) ** (-0.5)
    core, xh, y, z = (lax.axis_index(a) for a in ("core", "xh", "y", "z"))
    nz, ny, nxl = lax.axis_size("z"), lax.axis_size("y"), lax.axis_size("xl")
    half = toks // 2
    at = jnp.stack([core, xh, y, z]).astype(jnp.int32)

    block = jnp.concatenate(
        [
            latent,
            (positions // 64).astype(BF16)[:, None],
            (positions % 64).astype(BF16)[:, None],
            jnp.zeros((toks, LANES - lat - rope - 2), BF16),
        ],
        axis=1,
    )
    mine = lax.dynamic_slice_in_dim(block, core * half, half, 0)
    near = [shift(mine, CTX, by) for by in (1, 2, 3)]
    wt = w_o.T
    cols = wt.shape[0]
    xl = lax.axis_index("xl")
    w_other = shift(wt, "xl", 1)
    pair = jnp.where(xl == 0, jnp.stack([wt, w_other]), jnp.stack([w_other, wt]))
    pair = pair.reshape(nxl * cols, wt.shape[1])
    q_lat = jnp.einsum("thn,hnl->lht", q_nope, w_uk, preferred_element_type=F32).astype(BF16)
    q_rot = q_rope.reshape(toks, heads, rope).transpose(2, 1, 0)
    q = jnp.concatenate(
        [q_lat, q_rot, jnp.zeros((LANES - lat - rope, heads, toks), BF16)], axis=0
    ).reshape(LANES, heads * toks)
    qpos = positions.astype(F32)[None, :]

    *near, q, w_uv, pair = lax.optimization_barrier((*near, q, w_uv, pair))
    have = jnp.concatenate([mine, *near], axis=0)
    four = shift(have, CTX, 4)
    eight = shift(have, CTX, 8)
    twelve = shift(four, CTX, 8)
    swap = lambda a: shift(a, "core", 1)

    ring = [pair] + [None] * (nz - 1)
    up = down = pair
    for s in range(1, nz // 2 + 1):
        down = ring[s] = shift(down, "z", -1)
        if s < nz // 2:
            up = ring[nz - s] = shift(up, "z", 1)

    go = functools.partial(attention, q, qpos, scale=scale, lat=lat)
    state = go([have, swap(have)], None, None, name="attend_a")
    state = go([four, swap(four), eight, swap(eight)], state, None, name="attend_b")
    (h,) = go([twelve, swap(twelve)], state, w_uv, name="attend_c")

    h_at = [h] + [shift(h, "y", r) for r in range(1, ny)]
    wid, hv = nz * nxl * cols, heads * w_uv.shape[2]
    (w_all,) = call(functools.partial(gather_w, nz), [at, *ring], [((wid, hv), BF16)], "gather_w")
    rows = toks // 4
    pieces = [None] * ny
    for group in ((0,), (1, 2, 3)):
        k = len(group)
        if group[0]:
            *got, give = lax.optimization_barrier((*[h_at[r] for r in group], give))
            for r, g in zip(group, got):
                h_at[r] = g
        keep, give = call(
            functools.partial(project, k),
            [at, *[h_at[r] for r in group], w_all],
            [((k, 2, rows, wid), F32), ((k, 2, rows, wid), BF16)],
            f"project_{group[0]}",
            [pltpu.VMEM((k * toks, wid), F32)],
        )
        keep, give = call(
            fold, [at, keep, swap(give)], [((k, rows, wid), F32), ((k, rows, wid), BF16)], f"fold_{group[0]}"
        )
        done = (keep + shift(give, "xh", 1).astype(F32)).astype(BF16)
        for i, r in enumerate(group):
            pieces[r] = done[i] if r == 0 else shift(done[i], "y", -r)
    (out,) = call(
        functools.partial(finish, nz, ny),
        [at, *pieces],
        [((rows, wid * ny), BF16)],
        "finish",
        [pltpu.VMEM((ny, rows, wid), F32)],
    )
    return out


def solution(mesh):
    fine = Mesh(mesh.devices.reshape(8, 4, 2, 2, 2), (*CTX, *HEAD))
    placed = (
        P(CTX, HEAD, None),
        P(CTX, HEAD),
        P(CTX, None),
        P(CTX),
        P(HEAD, None, None),
        P(HEAD, None, None),
        P(HEAD, CTX),
    )
    return jax.shard_map(
        local, mesh=fine, in_specs=placed, out_specs=P((*CTX, *HEAD), None), check_vma=False
    )
```
